32 devices in a mesh: seq: 8 (over z, y), head: 4 (over x, core).
Axes of the slice: x: 2, y: 2, z: 4, core: 2. Of those that a mesh axis runs over, the one named last changes fastest.
Arguments:
- tokens: bfloat16 [16384, 1024], P('seq', 'head'), may hold values from -32 to 32
- buckets: int32 [128, 16], P('seq', 'head'), may hold values from 0 to 63, as said below
- w_shared: bfloat16 [1024, 1024], P(None, 'head'), may hold values from -3 to 3
- w_value: bfloat16 [1024, 1024], P(None, 'head'), may hold values from -0.1875 to 0.1875
- w_output: bfloat16 [1024, 1024], P(None, 'head'), may hold values from -0.1875 to 0.1875
Outputs:
- mixed_out: bfloat16 [16384, 1024], P('seq', 'head')
The draws below stay inside these ranges and needn't reach their ends.
Inputs may be any that keep to these rules, and one draw needn't show every extreme that they name: `buckets`: for each head, the ids 0 to 63 all occur. With the owner of a block in head h being its position in head h's ordering integer-divided by 16, exactly 16 blocks of each head fall to each owner, and over the 4 heads held by one device along `head` the 16 blocks held by one device along `seq` fall at most 8 to any one owner; 8 is reached in every draw.
All inputs are finite; a program needn't handle non-finite values.
Results may differ from the reference program's by a relative error of at most 0.012.
The reference program's roundings to bfloat16 on the way (of `shared`, `values`, `khat`, `weights` and `attention`) count: a program that leaves them out, or rounds other values in their place, can miss the bound.
Values may be sent and summed in bfloat16 or wider, within the bound.
A program may use at most 64 MiB of HBM per device.

```python
import jax
import jax.numpy as jnp
from jax import lax

D = 1024
H = 16
DH = 64
BLK = 128
HPD = 4
BLK_DEV = 16
TOTAL_BLOCKS = 128
TOKENS = 16384
NBUCK = 64
N_SEQ = 8
N_HEAD = 4


def draw_tokens(key, part):
    base = jnp.clip(jax.random.normal(jax.random.fold_in(key, 101), (TOKENS, D), jnp.float32), -6.0, 6.0)
    return base.astype(jnp.bfloat16)


def draw_w_shared(key, part):
    weight = jnp.clip(jax.random.normal(jax.random.fold_in(key, 201), (D, D), jnp.float32), -6.0, 6.0) * D ** (-0.5)
    weight = jnp.clip(weight, -3.0, 3.0)
    return weight.astype(jnp.bfloat16)


def draw_buckets(key, part):
    item_count = BLK_DEV * HPD
    span = max(item_count, N_SEQ)
    group_keys = jax.random.split(jax.random.fold_in(key, 11), N_HEAD)
    offsets = jax.vmap(lambda gkey: jax.random.permutation(gkey, span)[:item_count])(group_keys) % N_SEQ
    offsets = offsets.reshape(H, BLK_DEV).astype(jnp.int32)
    source = jnp.arange(N_SEQ, dtype=jnp.int32)
    owner_index = (source[None, :, None] + offsets[:, None, :]) % N_SEQ
    senders = (owner_index[:, :, :, None] - offsets[:, None, None, :]) % N_SEQ
    sender_key = senders * BLK_DEV + jnp.arange(BLK_DEV, dtype=jnp.int32)[None, None, None, :]
    own_key = source[None, :, None] * BLK_DEV + jnp.arange(BLK_DEV, dtype=jnp.int32)[None, None, :]
    rank_order = jnp.sum((sender_key < own_key[..., None]).astype(jnp.int32), axis=-1)
    position = (owner_index * BLK_DEV + rank_order).reshape(H, TOTAL_BLOCKS)
    head_rows = jnp.arange(H, dtype=jnp.int32)[:, None]
    block_ids = jnp.broadcast_to(jnp.arange(TOTAL_BLOCKS, dtype=jnp.int32)[None, :], (H, TOTAL_BLOCKS))
    sorted_block = jnp.zeros((H, TOTAL_BLOCKS), jnp.int32).at[head_rows, position].set(block_ids)
    forced = jnp.concatenate([jnp.zeros((H, 1), bool), sorted_block[:, 1:] < sorted_block[:, :-1]], axis=1)
    scoring_keys = jax.random.split(jax.random.fold_in(key, 12), H)
    score_matrix = jax.vmap(lambda sorted_key: jax.random.permutation(sorted_key, TOTAL_BLOCKS))(scoring_keys).astype(jnp.int32)
    score_matrix = jnp.where(forced, score_matrix + TOTAL_BLOCKS, score_matrix)
    score_matrix = score_matrix.at[:, 0].set(-1)
    picked = lax.top_k(score_matrix, NBUCK - 1)[1].astype(jnp.int32)
    breaks = jnp.zeros((H, TOTAL_BLOCKS), jnp.int32).at[head_rows, picked].set(1)
    labels = jnp.cumsum(breaks, axis=1).astype(jnp.int32)
    bucket_ids = jnp.take_along_axis(labels, position, axis=1)
    return jnp.transpose(bucket_ids).astype(jnp.int32)


def shard_levels(key, extent, cuts, low, top_value):
    level, own = 1.0, jax.random.fold_in(key, 6)
    for axis_at, blocks in cuts:
        heights = jnp.exp(jax.random.uniform(jax.random.fold_in(own, axis_at), (blocks,), jnp.float32, low / len(cuts), top_value / len(cuts)))
        level = level * jnp.repeat(heights, extent[axis_at] // blocks).reshape([-1 if axis == axis_at else 1 for axis in range(len(extent))])
    return level


def centred(key, shape, spread, limit, cuts=(), held_as=jnp.bfloat16):
    factor_of = shard_levels(key, shape, cuts, -0.22, 0.18) if cuts else 1.0
    drawn = jax.random.normal(key, shape, jnp.float32) * spread * factor_of
    return jnp.minimum(jnp.maximum(drawn, -limit), limit).astype(held_as)


def setup_inputs(seed: int = 0) -> dict:
    key_of = jax.random.split(jax.random.key(seed), 6)
    tokens = draw_tokens(jax.random.fold_in(key_of[5], 71), 0)
    buckets = draw_buckets(jax.random.fold_in(key_of[5], 71), 0)
    w_shared = draw_w_shared(jax.random.fold_in(key_of[5], 71), 0)
    w_value = centred(key_of[3], (D, D), D ** -0.5, 0.1875, ((1, 4),))
    w_output = centred(key_of[4], (D, D), D ** -0.5, 0.1875, ((1, 4),))
    return dict(tokens=tokens, buckets=buckets, w_shared=w_shared, w_value=w_value, w_output=w_output)


def attend(sorted_shared, value_sorted):
    preceding_s = jnp.roll(sorted_shared, 1, axis=0)
    preceding_v = jnp.roll(value_sorted, 1, axis=0)
    key_shared = jnp.concatenate([preceding_s, sorted_shared], axis=1)
    key_values = jnp.concatenate([preceding_v, value_sorted], axis=1)
    key_float = key_shared.astype(jnp.float32)
    khat = (key_float * lax.rsqrt(lax.optimization_barrier(jnp.mean(key_float * key_float, axis=-1, keepdims=True)) + 1e-06)).astype(jnp.bfloat16)
    scores = jnp.einsum('nqd,nkd->nqk', sorted_shared.astype(jnp.float32), khat.astype(jnp.float32)) * DH ** (-0.5)
    self_mask = jnp.arange(2 * BLK)[None, :] == jnp.arange(BLK)[:, None] + BLK
    scores = jnp.where(self_mask[None], jnp.float32(-100000.0), scores)
    row_max = lax.optimization_barrier(jnp.max(scores, axis=-1, keepdims=True))
    expo = jnp.exp(scores - row_max)
    weights = (expo / lax.optimization_barrier(jnp.sum(expo, axis=-1, keepdims=True))).astype(jnp.bfloat16)
    return jnp.einsum('nqk,nkd->nqd', weights.astype(jnp.float32), key_values.astype(jnp.float32)).astype(jnp.bfloat16)

def reference(tokens, buckets, w_shared, w_value, w_output):

    def one_head(head_id):
        start = (head_id * DH).astype(jnp.int32)
        head_cols = lax.dynamic_slice_in_dim(w_shared, start, DH, 1)
        value_cols = lax.dynamic_slice_in_dim(w_value, start, DH, 1)
        shared = jnp.dot(tokens, head_cols, preferred_element_type=jnp.float32).astype(jnp.bfloat16)
        values = jnp.dot(tokens, value_cols, preferred_element_type=jnp.float32).astype(jnp.bfloat16)
        ordering = jnp.argsort(jnp.take(buckets, head_id, axis=1), stable=True).astype(jnp.int32)
        sorted_shared = shared.reshape(TOTAL_BLOCKS, BLK, DH)[ordering]
        value_sorted = values.reshape(TOTAL_BLOCKS, BLK, DH)[ordering]
        result = attend(sorted_shared, value_sorted)
        placed = jnp.zeros_like(result).at[ordering].set(result)
        return placed.reshape(TOKENS, DH)
    per_head = lax.map(one_head, jnp.arange(H, dtype=jnp.int32))
    attention = jnp.transpose(per_head, (1, 0, 2)).reshape(TOKENS, D)
    mixed = tokens.astype(jnp.float32) + jnp.dot(attention, w_output, preferred_element_type=jnp.float32)
    return mixed.astype(jnp.bfloat16)
```

```python
import functools

import jax
import jax.numpy as jnp
from jax import lax
from jax.experimental import pallas as pl
from jax.experimental.pallas import tpu as pltpu
from jax.sharding import PartitionSpec as P

DH = 64
BLK = 128
HG = 4
CH = 256
MESH = pl.DeviceIdType.MESH


def head_ring():
    g = lax.axis_index("head")
    h1 = g + 1 - 2 * lax.rem(g, 2)
    h2 = g + 2 - 4 * lax.div(g, 2)
    h3 = h1 + 2 - 4 * lax.div(h1, 2)
    return g, h1, h2, h3


def remote(src, dst, send, recv, seq, head):
    return pltpu.make_async_remote_copy(
        src_ref=src, dst_ref=dst, send_sem=send, recv_sem=recv,
        device_id=(seq, head), device_id_type=MESH,
    )


def greet(n, i, g, h1, h2):
    barrier = pltpu.get_barrier_semaphore()

    def say(p, c):
        pl.semaphore_signal(barrier, inc=1, device_id=(lax.rem(i + p, n), g), device_id_type=MESH)
        return c

    lax.fori_loop(1, n, say, 0)
    for h in (h1, h2):
        pl.semaphore_signal(barrier, inc=1, device_id=(i, h), device_id_type=MESH)
    pl.semaphore_wait(barrier, n + 1)


def project_kernel(n, nc, tok, buck, ws, wv, items, ball, g1, g2, g3, ids,
                   s1, r1, s2, r2, s3, r3, sb, rb, sh, rh):
    i = lax.axis_index("seq")
    g, h1, h2, h3 = head_ring()
    greet(n, i, g, h1, h2)

    def over_x(c):
        return remote(tok.at[c], g2.at[c], s2.at[c], r2.at[c], i, h2)

    def over_core(c):
        return remote(tok.at[c], g1.at[c], s1.at[c], r1.at[c], i, h1)

    def onward(c):
        return remote(g2.at[c], g3.at[c], s3.at[c], r3.at[c], i, h1)

    def launch(c, carry):
        over_x(c).start()
        over_core(c).start()
        return carry

    lax.fori_loop(0, nc, launch, 0)
    ids[0, i] = buck[...]

    def bucket_copy(p):
        peer = lax.rem(i + p, n)
        return remote(buck, ids.at[0, i], sb.at[peer], rb.at[i], peer, g)

    def bucket_start(p, carry):
        bucket_copy(p).start()
        return carry

    lax.fori_loop(1, n, bucket_start, 0)

    def bucket_wait(p, carry):
        src = lax.rem(i + n - p, n)
        remote(buck, ids.at[0, src], sb.at[src], rb.at[src], src, g).wait_recv()
        return carry

    lax.fori_loop(1, n, bucket_wait, 0)
    id1 = remote(ids.at[0], ids.at[1], sh.at[0], rh.at[0], i, h1)
    id2 = remote(ids.at[0], ids.at[2], sh.at[1], rh.at[1], i, h2)
    id3 = remote(ids.at[2], ids.at[3], sh.at[2], rh.at[2], i, h1)
    id1.start()
    id2.start()

    def forward(c):
        over_x(c).wait_recv()
        onward(c).start()

    def compute(c):
        over_core(c).wait_recv()
        onward(c).wait_recv()
        shared = jnp.zeros((CH, HG * DH), jnp.float32)
        value = jnp.zeros((CH, HG * DH), jnp.float32)
        for ref, h in ((tok, g), (g1, h1), (g2, h2), (g3, h3)):
            x = ref[c]
            at = pl.ds(pl.multiple_of(h * CH, CH), CH)
            shared += jnp.dot(x, ws[at, :], preferred_element_type=jnp.float32)
            value += jnp.dot(x, wv[at, :], preferred_element_type=jnp.float32)
        shared = shared.astype(jnp.bfloat16)
        value = value.astype(jnp.bfloat16)
        for b in range(CH // BLK):
            for h in range(HG):
                rows, cols = slice(b * BLK, (b + 1) * BLK), slice(h * DH, (h + 1) * DH)
                items[(c * (CH // BLK) + b) * HG + h] = jnp.concatenate(
                    [shared[rows, cols], value[rows, cols]], axis=1)

    forward(0)

    def step(c, carry):
        forward(c)
        compute(c - 1)
        return carry

    lax.fori_loop(1, nc, step, 0)
    id2.wait_recv()
    id3.start()
    compute(nc - 1)
    id1.wait_recv()
    id3.wait_recv()
    ball[...] = ids[...]

    def drain(c, carry):
        over_x(c).wait_send()
        over_core(c).wait_send()
        onward(c).wait_send()
        return carry

    lax.fori_loop(0, nc, drain, 0)

    def bucket_drain(p, carry):
        bucket_copy(p).wait_send()
        return carry

    lax.fori_loop(1, n, bucket_drain, 0)
    id1.wait_send()
    id2.wait_send()
    id3.wait_send()


def attend_kernel(n, cap, nb, idx, items, tok, wo, out, outbox, inbox, tail_out, tail_in, out2, ans,
                  sa, ra, st, rt, sr, rr, s1, r1, s2, r2, s3, r3):
    i = lax.axis_index("seq")
    g, h1, h2, h3 = head_ring()
    slots = n * cap
    at_pred, at_tail, at_target = slots, 2 * slots, 2 * slots + HG
    greet(n, i, g, h1, h2)

    def chunk(o):
        return pl.ds(o * cap, cap)

    def outward(p):
        peer = lax.rem(i + p, n)
        return remote(outbox.at[peer], inbox.at[chunk(i)], sa.at[peer], ra.at[i], peer, g)

    def pack(p, carry):
        peer = lax.rem(i + p, n)
        for k in range(cap):
            outbox[peer, k] = items[idx[peer * cap + k]]
        outward(p).start()
        return carry

    lax.fori_loop(1, n, pack, 0)
    for k in range(cap):
        inbox[i * cap + k] = items[idx[i * cap + k]]
    for h in range(HG):
        inbox[slots + h] = jnp.zeros((BLK, 2 * DH), jnp.bfloat16)

    def arrive(p, carry):
        src = lax.rem(i + n - p, n)
        remote(outbox.at[src], inbox.at[chunk(src)], sa.at[src], ra.at[src], src, g).wait_recv()
        return carry

    lax.fori_loop(1, n, arrive, 0)
    for h in range(HG):
        tail_out[h] = inbox[idx[at_tail + h]]
    tail = remote(tail_out, tail_in, st.at[0], rt.at[0], lax.rem(i + 1, n), g)
    tail.start()
    tail.wait_recv()
    for h in range(HG):
        inbox[slots + h] = tail_in[h]

    lane = lax.broadcasted_iota(jnp.int32, (1, 2 * DH), 1)
    is_key = (lane < DH).astype(jnp.float32)
    row_at = lax.broadcasted_iota(jnp.int32, (BLK, 2 * BLK), 0)
    col_at = lax.broadcasted_iota(jnp.int32, (BLK, 2 * BLK), 1)
    itself = col_at == row_at + BLK

    def attend(j):
        own = inbox[j]
        keys = jnp.concatenate([inbox[idx[at_pred + j]], own], axis=0)
        query = (own.astype(jnp.float32) * (is_key * (DH ** -0.5))).astype(jnp.bfloat16)
        kf = keys.astype(jnp.float32) * is_key
        square = jnp.sum(kf * kf, axis=1, keepdims=True) * (1.0 / DH)
        khat = (kf * lax.rsqrt(square + 1e-6)).astype(jnp.bfloat16)
        scores = lax.dot_general(query, khat, (((1,), (1,)), ((), ())),
                                 preferred_element_type=jnp.float32)
        scores = jnp.where(itself, jnp.float32(-100000.0), scores)
        expo = jnp.exp(scores - jnp.max(scores, axis=1, keepdims=True))
        weights = (expo * (1.0 / jnp.sum(expo, axis=1, keepdims=True))).astype(jnp.bfloat16)
        mixed = jnp.dot(weights, keys, preferred_element_type=jnp.float32).astype(jnp.bfloat16)
        return jnp.concatenate([mixed[: BLK // 2, DH:], mixed[BLK // 2:, DH:]], axis=1)

    def reply(p):
        peer = lax.rem(i + p, n)
        return remote(out2.at[peer], ans.at[0, chunk(i)], sr.at[peer], rr.at[i], peer, g)

    def relay1(o):
        return remote(ans.at[0, chunk(o)], ans.at[1, chunk(o)], s1.at[o], r1.at[o], i, h1)

    def relay2(o):
        return remote(ans.at[0, chunk(o)], ans.at[2, chunk(o)], s2.at[o], r2.at[o], i, h2)

    def relay3(o):
        return remote(ans.at[2, chunk(o)], ans.at[3, chunk(o)], s3.at[o], r3.at[o], i, h1)

    for k in range(cap):
        ans[0, i * cap + k] = attend(i * cap + k)
    relay2(i).start()
    relay1(i).start()

    def answer(p, carry):
        peer = lax.rem(i + p, n)
        for k in range(cap):
            out2[peer, k] = attend(peer * cap + k)
        reply(p).start()
        return carry

    lax.fori_loop(1, n, answer, 0)

    def relay(p, carry):
        src = lax.rem(i + n - p, n)
        remote(out2.at[src], ans.at[0, chunk(src)], sr.at[src], rr.at[src], src, g).wait_recv()
        relay2(src).start()
        relay1(src).start()
        before = lax.rem(i + n - p + 1, n)
        relay2(before).wait_recv()
        relay3(before).start()
        return carry

    lax.fori_loop(1, n, relay, 0)
    last = lax.rem(i + 1, n)
    relay2(last).wait_recv()
    relay3(last).start()

    def settle(o, carry):
        relay1(o).wait_recv()
        relay3(o).wait_recv()
        return carry

    lax.fori_loop(0, n, settle, 0)

    group = 4

    def finish(q, carry):
        total = jnp.zeros((group * BLK, wo.shape[1]), jnp.float32)
        for r, h in enumerate((g, h1, h2, h3)):
            rows = []
            for b in range(group):
                at = at_target + (r * nb + q * group + b) * HG
                parts = [ans[r, idx[at + k]] for k in range(HG)]
                rows.append(jnp.concatenate([x[:, :DH] for x in parts], axis=1))
                rows.append(jnp.concatenate([x[:, DH:] for x in parts], axis=1))
            total += jnp.dot(jnp.concatenate(rows, axis=0),
                             wo[pl.ds(pl.multiple_of(h * HG * DH, HG * DH), HG * DH), :],
                             preferred_element_type=jnp.float32)
        at = pl.ds(q * group, group)
        base = tok[at].reshape(group * BLK, -1).astype(jnp.float32)
        out[at] = (base + total).astype(jnp.bfloat16).reshape(group, BLK, -1)
        return carry

    lax.fori_loop(0, nb // group, finish, 0)

    def drain(p, carry):
        outward(p).wait_send()
        reply(p).wait_send()
        return carry

    lax.fori_loop(1, n, drain, 0)
    tail.wait_send()

    def drain_relays(o, carry):
        relay1(o).wait_send()
        relay2(o).wait_send()
        relay3(o).wait_send()
        return carry

    lax.fori_loop(0, n, drain_relays, 0)


def index_tables(ball, n, nb, cap):
    i = lax.axis_index("seq")
    blocks, slots = n * nb, n * cap
    key = ball[..., :HG].reshape(HG, blocks, HG) * blocks + jnp.arange(blocks, dtype=jnp.int32)[None, :, None]
    key = jnp.transpose(key, (0, 2, 1))
    position = jnp.sum((key[:, :, None, :] < key[:, :, :, None]).astype(jnp.int32), axis=3)
    position = jnp.transpose(position, (0, 2, 1)).reshape(HG, n, nb * HG)
    count = nb * HG
    item = jnp.arange(count, dtype=jnp.int32)
    owner, within = position // nb, position % nb
    same = owner[..., :, None] == owner[..., None, :]
    slot = jnp.sum((same & (item[None, :] < item[:, None])).astype(jnp.int32), axis=3)
    target = lax.dynamic_index_in_dim(owner * cap + slot, i, 1, keepdims=False)
    slot_ids = jnp.arange(slots, dtype=jnp.int32)
    inverse = jnp.sum(jnp.where(target[0][None, :] == slot_ids[:, None], item[None, :], 0), axis=1)
    place = (jnp.arange(n, dtype=jnp.int32)[:, None] * cap + slot[0]).reshape(-1)
    mine = (owner[0] == i).reshape(-1)
    grid = ((item % HG)[None, :] * nb + within[0]).reshape(-1)
    grid_of = jnp.sum(jnp.where(mine & (place == slot_ids[:, None]), grid, 0), axis=1)
    slot_of = jnp.sum(jnp.where(mine & (grid == item[:, None]), place, 0), axis=1)
    inside = jnp.sum(jnp.where(item[None, :] == grid_of[:, None] - 1, slot_of[None, :], 0), axis=1)
    before = jnp.where(grid_of % nb == 0, slots + grid_of // nb, inside)
    tails = slot_of.reshape(HG, nb)[:, nb - 1]
    return jnp.concatenate([inverse, before, tails, target.reshape(-1)]).astype(jnp.int32)


def per_device(tokens, buckets, w_shared, w_value, w_output):
    n = lax.axis_size("seq")
    nb = buckets.shape[0]
    rows, width = tokens.shape
    cap = max(1, nb * HG // n)
    nc = rows // CH
    vmem = pl.BlockSpec(memory_space=pltpu.VMEM)
    dma = lambda k: pltpu.SemaphoreType.DMA((k,))
    bf = jnp.bfloat16
    padded = jnp.pad(buckets, ((0, 0), (0, 128 - HG)))
    items, ball = pl.pallas_call(
        functools.partial(project_kernel, n, nc),
        out_shape=(jax.ShapeDtypeStruct((nb * HG, BLK, 2 * DH), bf),
                   jax.ShapeDtypeStruct((HG, n, nb, 128), jnp.int32)),
        in_specs=[vmem] * 4,
        out_specs=(vmem, vmem),
        scratch_shapes=[pltpu.VMEM((nc, CH, width), bf)] * 3
        + [pltpu.VMEM((HG, n, nb, 128), jnp.int32)]
        + [dma(nc)] * 6 + [dma(n), dma(n), dma(3), dma(3)],
        compiler_params=pltpu.CompilerParams(collective_id=0, has_side_effects=True,
                                             vmem_limit_bytes=40 << 20),
    )(tokens.reshape(nc, CH, width), padded, w_shared, w_value)
    idx = index_tables(ball, n, nb, cap)
    slots = n * cap
    out = pl.pallas_call(
        functools.partial(attend_kernel, n, cap, nb),
        out_shape=jax.ShapeDtypeStruct((nb, BLK, width), bf),
        in_specs=[pl.BlockSpec(memory_space=pltpu.SMEM)] + [vmem] * 3,
        out_specs=vmem,
        scratch_shapes=[
            pltpu.VMEM((n, cap, BLK, 2 * DH), bf),
            pltpu.VMEM((slots + HG, BLK, 2 * DH), bf),
            pltpu.VMEM((HG, BLK, 2 * DH), bf),
            pltpu.VMEM((HG, BLK, 2 * DH), bf),
            pltpu.VMEM((n, cap, BLK // 2, 2 * DH), bf),
            pltpu.VMEM((HG, slots, BLK // 2, 2 * DH), bf),
        ] + [dma(n), dma(n), dma(1), dma(1), dma(n), dma(n)] + [dma(n)] * 6,
        compiler_params=pltpu.CompilerParams(collective_id=1, has_side_effects=True,
                                             vmem_limit_bytes=40 << 20),
    )(idx, items, tokens.reshape(nb, BLK, width), w_output)
    return out.reshape(rows, width)


def solution(mesh):
    return jax.shard_map(
        per_device,
        mesh=mesh,
        in_specs=(
            P("seq", "head"),
            P("seq", "head"),
            P(None, "head"),
            P(None, "head"),
            P(None, "head"),
        ),
        out_specs=P("seq", "head"),
        check_vma=False,
    )
```

```python
import functools

import jax
import jax.numpy as jnp
from jax import lax
from jax.experimental import pallas as pl
from jax.experimental.pallas import tpu as pltpu
from jax.sharding import PartitionSpec as P

DH = 64
BLK = 128
HG = 4
CH = 256
MESH = pl.DeviceIdType.MESH


def head_ring():
    g = lax.axis_index("head")
    h1 = g + 1 - 2 * lax.rem(g, 2)
    h2 = g + 2 - 4 * lax.div(g, 2)
    h3 = h1 + 2 - 4 * lax.div(h1, 2)
    return g, h1, h2, h3


def remote(src, dst, send, recv, seq, head):
    return pltpu.make_async_remote_copy(
        src_ref=src, dst_ref=dst, send_sem=send, recv_sem=recv,
        device_id=(seq, head), device_id_type=MESH,
    )


def greet(n, i, g, h1, h2):
    barrier = pltpu.get_barrier_semaphore()

    def say(p, c):
        pl.semaphore_signal(barrier, inc=1, device_id=(lax.rem(i + p, n), g), device_id_type=MESH)
        return c

    lax.fori_loop(1, n, say, 0)
    for h in (h1, h2):
        pl.semaphore_signal(barrier, inc=1, device_id=(i, h), device_id_type=MESH)
    pl.semaphore_wait(barrier, n + 1)


def project_kernel(n, nc, tok, buck, ws_hbm, wv_hbm, items_s, items_v, ball, own, ws, wv, g1, g2, g3, ids,
                   local, s1, r1, s2, r2, s3, r3, sb, rb, sh, rh):
    i = lax.axis_index("seq")
    g, h1, h2, h3 = head_ring()
    loads = [pltpu.make_async_copy(src, dst, local.at[k])
             for k, (src, dst) in enumerate(((tok, own), (ws_hbm, ws), (wv_hbm, wv)))]
    for load in loads:
        load.start()
    greet(n, i, g, h1, h2)

    def over_x(c):
        return remote(tok.at[c], g2.at[c], s2.at[c], r2.at[c], i, h2)

    def over_core(c):
        return remote(tok.at[c], g1.at[c], s1.at[c], r1.at[c], i, h1)

    def onward(c):
        return remote(g2.at[c], g3.at[c], s3.at[c], r3.at[c], i, h1)

    def launch(c, carry):
        over_x(c).start()
        over_core(c).start()
        return carry

    lax.fori_loop(0, nc, launch, 0)
    ids[0, i] = buck[...]

    def bucket_copy(p):
        peer = lax.rem(i + p, n)
        return remote(buck, ids.at[0, i], sb.at[peer], rb.at[i], peer, g)

    def bucket_start(p, carry):
        bucket_copy(p).start()
        return carry

    lax.fori_loop(1, n, bucket_start, 0)

    def bucket_wait(p, carry):
        src = lax.rem(i + n - p, n)
        remote(buck, ids.at[0, src], sb.at[src], rb.at[src], src, g).wait_recv()
        return carry

    lax.fori_loop(1, n, bucket_wait, 0)
    id1 = remote(ids.at[0], ids.at[1], sh.at[0], rh.at[0], i, h1)
    id2 = remote(ids.at[0], ids.at[2], sh.at[1], rh.at[1], i, h2)
    id3 = remote(ids.at[2], ids.at[3], sh.at[2], rh.at[2], i, h1)
    id1.start()
    id2.start()

    def forward(c):
        over_x(c).wait_recv()
        onward(c).start()

    def compute(c):
        over_core(c).wait_recv()
        onward(c).wait_recv()
        shared = jnp.zeros((CH, HG * DH), jnp.float32)
        value = jnp.zeros((CH, HG * DH), jnp.float32)
        for ref, h in ((own, g), (g1, h1), (g2, h2), (g3, h3)):
            x = ref[c]
            at = pl.ds(pl.multiple_of(h * CH, CH), CH)
            shared += jnp.dot(x, ws[at, :], preferred_element_type=jnp.float32)
            value += jnp.dot(x, wv[at, :], preferred_element_type=jnp.float32)
        for full, dst in ((shared.astype(jnp.bfloat16), items_s), (value.astype(jnp.bfloat16), items_v)):
            for b in range(CH // BLK):
                for h in range(HG):
                    cols = slice(h * DH, (h + 1) * DH)
                    dst[(c * (CH // BLK) + b) * HG + h] = jnp.concatenate(
                        [full[b * BLK: b * BLK + BLK // 2, cols],
                         full[b * BLK + BLK // 2: (b + 1) * BLK, cols]], axis=1)

    for load in loads:
        load.wait()
    forward(0)

    def step(c, carry):
        forward(c)
        compute(c - 1)
        return carry

    lax.fori_loop(1, nc, step, 0)
    id2.wait_recv()
    id3.start()
    compute(nc - 1)
    id1.wait_recv()
    id3.wait_recv()
    ball[...] = ids[...]

    def drain(c, carry):
        over_x(c).wait_send()
        over_core(c).wait_send()
        onward(c).wait_send()
        return carry

    lax.fori_loop(0, nc, drain, 0)

    def bucket_drain(p, carry):
        bucket_copy(p).wait_send()
        return carry

    lax.fori_loop(1, n, bucket_drain, 0)
    id1.wait_send()
    id2.wait_send()
    id3.wait_send()


def attend_kernel(n, cap, nb, idx, items_s, items_v, tok, wo, out, s_out, v_out, s_in, v_in,
                  ts_out, ts_in, tv_out, tv_in, qbuf, kbuf, vbuf, wbuf, out2, ans,
                  sa, ra, sv, rv, st, rt, sr, rr, s1, r1, s2, r2, s3, r3):
    i = lax.axis_index("seq")
    g, h1, h2, h3 = head_ring()
    slots = n * cap
    at_pred, at_tail, at_target = slots, 2 * slots, 2 * slots + HG
    greet(n, i, g, h1, h2)

    def chunk(o):
        return pl.ds(o * cap, cap)

    def send_s(p):
        peer = lax.rem(i + p, n)
        return remote(s_out.at[peer], s_in.at[chunk(i)], sa.at[peer], ra.at[i], peer, g)

    def send_v(p):
        peer = lax.rem(i + p, n)
        return remote(v_out.at[peer], v_in.at[chunk(i)], sv.at[peer], rv.at[i], peer, g)

    def pack_s(p, carry):
        peer = lax.rem(i + p, n)
        for k in range(cap):
            s_out[peer, k] = items_s[idx[peer * cap + k]]
        send_s(p).start()
        return carry

    lax.fori_loop(1, n, pack_s, 0)

    def pack_v(p, carry):
        peer = lax.rem(i + p, n)
        for k in range(cap):
            v_out[peer, k] = items_v[idx[peer * cap + k]]
        return carry

    lax.fori_loop(1, n, pack_v, 0)
    for k in range(cap):
        s_in[i * cap + k] = items_s[idx[i * cap + k]]
        v_in[i * cap + k] = items_v[idx[i * cap + k]]

    low = lax.broadcasted_iota(jnp.int32, (BLK // 2, 2 * DH), 1) < DH
    query_scale = jnp.where(lax.broadcasted_iota(jnp.int32, (1, 2 * DH), 1) < DH,
                            jnp.float32(DH ** -0.5), jnp.float32(0.0))

    def unfold(x):
        x = x.astype(jnp.float32)
        turned = pltpu.roll(x, DH, 1)
        return jnp.concatenate([jnp.where(low, x, turned), jnp.where(low, turned, x)], axis=0)

    def khat_of(x):
        square = jnp.sum(x * x, axis=1, keepdims=True) * (0.5 / DH)
        return (x * lax.rsqrt(square + 1e-6)).astype(jnp.bfloat16)

    def ready_s(o):
        for k in range(cap):
            j = o * cap + k
            x = unfold(s_in[j])
            qbuf[j] = (x * query_scale).astype(jnp.bfloat16)
            kbuf[j] = khat_of(x)

    def ready_v(o):
        for k in range(cap):
            j = o * cap + k
            vbuf[j] = unfold(v_in[j]).astype(jnp.bfloat16)

    ready_s(i)

    def arrive_s(p, carry):
        src = lax.rem(i + n - p, n)
        remote(s_out.at[src], s_in.at[chunk(src)], sa.at[src], ra.at[src], src, g).wait_recv()
        send_v(p).start()
        ready_s(src)
        return carry

    lax.fori_loop(1, n, arrive_s, 0)
    for h in range(HG):
        ts_out[h] = s_in[idx[at_tail + h]]
    following = lax.rem(i + 1, n)
    tail_s = remote(ts_out, ts_in, st.at[0], rt.at[0], following, g)
    tail_s.start()
    ready_v(i)
    tail_s.wait_recv()
    for h in range(HG):
        kbuf[slots + h] = khat_of(unfold(ts_in[h]))

    row_at = lax.broadcasted_iota(jnp.int32, (BLK, 2 * BLK), 0)
    col_at = lax.broadcasted_iota(jnp.int32, (BLK, 2 * BLK), 1)
    itself = col_at == row_at + BLK

    def weigh(o, carry):
        for k in range(cap):
            j = o * cap + k
            keys = jnp.concatenate([kbuf[idx[at_pred + j]], kbuf[j]], axis=0)
            scores = lax.dot_general(qbuf[j], keys, (((1,), (1,)), ((), ())),
                                     preferred_element_type=jnp.float32)
            scores = jnp.where(itself, jnp.float32(-100000.0), scores)
            expo = jnp.exp(scores - jnp.max(scores, axis=1, keepdims=True))
            wbuf[j] = (expo * (1.0 / jnp.sum(expo, axis=1, keepdims=True))).astype(jnp.bfloat16)
        return carry

    lax.fori_loop(0, n, weigh, 0)

    def arrive_v(p, carry):
        src = lax.rem(i + n - p, n)
        remote(v_out.at[src], v_in.at[chunk(src)], sv.at[src], rv.at[src], src, g).wait_recv()
        ready_v(src)
        return carry

    lax.fori_loop(1, n, arrive_v, 0)
    for h in range(HG):
        tv_out[h] = v_in[idx[at_tail + h]]
    tail_v = remote(tv_out, tv_in, st.at[1], rt.at[1], following, g)
    tail_v.start()
    tail_v.wait_recv()
    for h in range(HG):
        vbuf[slots + h] = unfold(tv_in[h]).astype(jnp.bfloat16)

    def attend(j):
        values = jnp.concatenate([vbuf[idx[at_pred + j]], vbuf[j]], axis=0)
        mixed = jnp.dot(wbuf[j], values, preferred_element_type=jnp.float32)
        return jnp.where(low, mixed[: BLK // 2], mixed[BLK // 2:]).astype(jnp.bfloat16)

    def reply(p):
        peer = lax.rem(i + p, n)
        return remote(out2.at[peer], ans.at[0, chunk(i)], sr.at[peer], rr.at[i], peer, g)

    def relay1(o):
        return remote(ans.at[0, chunk(o)], ans.at[1, chunk(o)], s1.at[o], r1.at[o], i, h1)

    def relay2(o):
        return remote(ans.at[0, chunk(o)], ans.at[2, chunk(o)], s2.at[o], r2.at[o], i, h2)

    def relay3(o):
        return remote(ans.at[2, chunk(o)], ans.at[3, chunk(o)], s3.at[o], r3.at[o], i, h1)

    for k in range(cap):
        ans[0, i * cap + k] = attend(i * cap + k)
    relay2(i).start()
    relay1(i).start()

    def answer(p, carry):
        peer = lax.rem(i + p, n)
        for k in range(cap):
            out2[peer, k] = attend(peer * cap + k)
        reply(p).start()
        return carry

    lax.fori_loop(1, n, answer, 0)

    def relay(p, carry):
        src = lax.rem(i + n - p, n)
        remote(out2.at[src], ans.at[0, chunk(src)], sr.at[src], rr.at[src], src, g).wait_recv()
        relay2(src).start()
        relay1(src).start()
        before = lax.rem(i + n - p + 1, n)
        relay2(before).wait_recv()
        relay3(before).start()
        return carry

    lax.fori_loop(1, n, relay, 0)
    last = lax.rem(i + 1, n)
    relay2(last).wait_recv()
    relay3(last).start()

    def settle(o, carry):
        relay1(o).wait_recv()
        relay3(o).wait_recv()
        return carry

    lax.fori_loop(0, n, settle, 0)

    group = 4

    def finish(q, carry):
        total = jnp.zeros((group * BLK, wo.shape[1]), jnp.float32)
        for r, h in enumerate((g, h1, h2, h3)):
            rows = []
            for b in range(group):
                at = at_target + (r * nb + q * group + b) * HG
                parts = [ans[r, idx[at + k]] for k in range(HG)]
                rows.append(jnp.concatenate([x[:, :DH] for x in parts], axis=1))
                rows.append(jnp.concatenate([x[:, DH:] for x in parts], axis=1))
            total += jnp.dot(jnp.concatenate(rows, axis=0),
                             wo[pl.ds(pl.multiple_of(h * HG * DH, HG * DH), HG * DH), :],
                             preferred_element_type=jnp.float32)
        at = pl.ds(q * group, group)
        base = tok[at].reshape(group * BLK, -1).astype(jnp.float32)
        out[at] = (base + total).astype(jnp.bfloat16).reshape(group, BLK, -1)
        return carry

    lax.fori_loop(0, nb // group, finish, 0)

    def drain(p, carry):
        send_s(p).wait_send()
        send_v(p).wait_send()
        reply(p).wait_send()
        return carry

    lax.fori_loop(1, n, drain, 0)
    tail_s.wait_send()
    tail_v.wait_send()

    def drain_relays(o, carry):
        relay1(o).wait_send()
        relay2(o).wait_send()
        relay3(o).wait_send()
        return carry

    lax.fori_loop(0, n, drain_relays, 0)


def index_tables(ball, n, nb, cap):
    i = lax.axis_index("seq")
    blocks, slots = n * nb, n * cap
    key = ball[..., :HG].reshape(HG, blocks, HG) * blocks + jnp.arange(blocks, dtype=jnp.int32)[None, :, None]
    key = jnp.transpose(key, (0, 2, 1))
    position = jnp.sum((key[:, :, None, :] < key[:, :, :, None]).astype(jnp.int32), axis=3)
    position = jnp.transpose(position, (0, 2, 1)).reshape(HG, n, nb * HG)
    count = nb * HG
    item = jnp.arange(count, dtype=jnp.int32)
    owner, within = position // nb, position % nb
    same = owner[..., :, None] == owner[..., None, :]
    slot = jnp.sum((same & (item[None, :] < item[:, None])).astype(jnp.int32), axis=3)
    target = lax.dynamic_index_in_dim(owner * cap + slot, i, 1, keepdims=False)
    slot_ids = jnp.arange(slots, dtype=jnp.int32)
    inverse = jnp.sum(jnp.where(target[0][None, :] == slot_ids[:, None], item[None, :], 0), axis=1)
    place = (jnp.arange(n, dtype=jnp.int32)[:, None] * cap + slot[0]).reshape(-1)
    mine = (owner[0] == i).reshape(-1)
    grid = ((item % HG)[None, :] * nb + within[0]).reshape(-1)
    grid_of = jnp.sum(jnp.where(mine & (place == slot_ids[:, None]), grid, 0), axis=1)
    slot_of = jnp.sum(jnp.where(mine & (grid == item[:, None]), place, 0), axis=1)
    inside = jnp.sum(jnp.where(item[None, :] == grid_of[:, None] - 1, slot_of[None, :], 0), axis=1)
    before = jnp.where(grid_of % nb == 0, slots + grid_of // nb, inside)
    tails = slot_of.reshape(HG, nb)[:, nb - 1]
    return jnp.concatenate([inverse, before, tails, target.reshape(-1)]).astype(jnp.int32)


def per_device(tokens, buckets, w_shared, w_value, w_output):
    n = lax.axis_size("seq")
    nb = buckets.shape[0]
    rows, width = tokens.shape
    cap = max(1, nb * HG // n)
    nc = rows // CH
    vmem = pl.BlockSpec(memory_space=pltpu.VMEM)
    dma = lambda k: pltpu.SemaphoreType.DMA((k,))
    bf = jnp.bfloat16
    padded = jnp.pad(buckets, ((0, 0), (0, 128 - HG)))
    hbm = pl.BlockSpec(memory_space=pl.ANY)
    half = (BLK // 2, 2 * DH)
    items_s, items_v, ball = pl.pallas_call(
        functools.partial(project_kernel, n, nc),
        out_shape=(jax.ShapeDtypeStruct((nb * HG,) + half, bf),
                   jax.ShapeDtypeStruct((nb * HG,) + half, bf),
                   jax.ShapeDtypeStruct((HG, n, nb, 128), jnp.int32)),
        in_specs=[hbm, vmem, hbm, hbm],
        out_specs=(vmem, vmem, vmem),
        scratch_shapes=[pltpu.VMEM((nc, CH, width), bf), pltpu.VMEM(w_shared.shape, bf), pltpu.VMEM(w_value.shape, bf)]
        + [pltpu.VMEM((nc, CH, width), bf)] * 3
        + [pltpu.VMEM((HG, n, nb, 128), jnp.int32)]
        + [dma(3)] + [dma(nc)] * 6 + [dma(n), dma(n), dma(3), dma(3)],
        compiler_params=pltpu.CompilerParams(collective_id=0, has_side_effects=True,
                                             vmem_limit_bytes=40 << 20),
    )(tokens.reshape(nc, CH, width), padded, w_shared, w_value)
    idx = index_tables(ball, n, nb, cap)
    slots = n * cap
    out = pl.pallas_call(
        functools.partial(attend_kernel, n, cap, nb),
        out_shape=jax.ShapeDtypeStruct((nb, BLK, width), bf),
        in_specs=[pl.BlockSpec(memory_space=pltpu.SMEM)] + [vmem] * 4,
        out_specs=vmem,
        scratch_shapes=[pltpu.VMEM((n, cap) + half, bf)] * 2
        + [pltpu.VMEM((slots,) + half, bf)] * 2
        + [pltpu.VMEM((HG,) + half, bf)] * 4
        + [pltpu.VMEM((slots, BLK, 2 * DH), bf)]
        + [pltpu.VMEM((slots + HG, BLK, 2 * DH), bf)] * 2
        + [pltpu.VMEM((slots, BLK, 2 * BLK), bf)]
        + [pltpu.VMEM((n, cap) + half, bf), pltpu.VMEM((HG, slots) + half, bf)]
        + [dma(n)] * 4 + [dma(2)] * 2 + [dma(n)] * 8,
        compiler_params=pltpu.CompilerParams(collective_id=1, has_side_effects=True,
                                             vmem_limit_bytes=48 << 20),
    )(idx, items_s, items_v, tokens.reshape(nb, BLK, width), w_output)
    return out.reshape(rows, width)


def solution(mesh):
    return jax.shard_map(
        per_device,
        mesh=mesh,
        in_specs=(
            P("seq", "head"),
            P("seq", "head"),
            P(None, "head"),
            P(None, "head"),
            P(None, "head"),
        ),
        out_specs=P("seq", "head"),
        check_vma=False,
    )
```

```python
import functools

import jax
import jax.numpy as jnp
from jax import lax
from jax.experimental import pallas as pl
from jax.experimental.pallas import tpu as pltpu
from jax.sharding import PartitionSpec as P

DH = 64
BLK = 128
HG = 4
CH = 256
MESH = pl.DeviceIdType.MESH


def head_ring():
    g = lax.axis_index("head")
    h1 = g + 1 - 2 * lax.rem(g, 2)
    h2 = g + 2 - 4 * lax.div(g, 2)
    h3 = h1 + 2 - 4 * lax.div(h1, 2)
    return g, h1, h2, h3


def remote(src, dst, send, recv, seq, head):
    return pltpu.make_async_remote_copy(
        src_ref=src, dst_ref=dst, send_sem=send, recv_sem=recv,
        device_id=(seq, head), device_id_type=MESH,
    )


def greet(n, i, g, h1, h2):
    barrier = pltpu.get_barrier_semaphore()

    def say(p, c):
        pl.semaphore_signal(barrier, inc=1, device_id=(lax.rem(i + p, n), g), device_id_type=MESH)
        return c

    lax.fori_loop(1, n, say, 0)
    for h in (h1, h2):
        pl.semaphore_signal(barrier, inc=1, device_id=(i, h), device_id_type=MESH)
    pl.semaphore_wait(barrier, n + 1)


def project_kernel(n, nc, tok, buck, ws_hbm, wv_hbm, items_s, items_v, ball, own, ws, wv, g1, g2, g3, ids,
                   local, s1, r1, s2, r2, s3, r3, sb, rb, sh, rh):
    i = lax.axis_index("seq")
    g, h1, h2, h3 = head_ring()
    loads = [pltpu.make_async_copy(src, dst, local.at[k])
             for k, (src, dst) in enumerate(((tok, own), (ws_hbm, ws), (wv_hbm, wv)))]
    for load in loads:
        load.start()
    greet(n, i, g, h1, h2)

    def over_x(c):
        return remote(tok.at[c], g2.at[c], s2.at[c], r2.at[c], i, h2)

    def over_core(c):
        return remote(tok.at[c], g1.at[c], s1.at[c], r1.at[c], i, h1)

    def onward(c):
        return remote(g2.at[c], g3.at[c], s3.at[c], r3.at[c], i, h1)

    def launch(c, carry):
        over_x(c).start()
        over_core(c).start()
        return carry

    lax.fori_loop(0, nc, launch, 0)
    ids[0, i] = buck[...]

    def bucket_copy(p):
        peer = lax.rem(i + p, n)
        return remote(buck, ids.at[0, i], sb.at[peer], rb.at[i], peer, g)

    def bucket_start(p, carry):
        bucket_copy(p).start()
        return carry

    lax.fori_loop(1, n, bucket_start, 0)

    def bucket_wait(p, carry):
        src = lax.rem(i + n - p, n)
        remote(buck, ids.at[0, src], sb.at[src], rb.at[src], src, g).wait_recv()
        return carry

    lax.fori_loop(1, n, bucket_wait, 0)
    id1 = remote(ids.at[0], ids.at[1], sh.at[0], rh.at[0], i, h1)
    id2 = remote(ids.at[0], ids.at[2], sh.at[1], rh.at[1], i, h2)
    id3 = remote(ids.at[2], ids.at[3], sh.at[2], rh.at[2], i, h1)
    id1.start()
    id2.start()

    def forward(c):
        over_x(c).wait_recv()
        onward(c).start()

    def compute(c):
        over_core(c).wait_recv()
        onward(c).wait_recv()
        shared = jnp.zeros((CH, HG * DH), jnp.float32)
        value = jnp.zeros((CH, HG * DH), jnp.float32)
        for ref, h in ((own, g), (g1, h1), (g2, h2), (g3, h3)):
            x = ref[c]
            at = pl.ds(pl.multiple_of(h * CH, CH), CH)
            shared += jnp.dot(x, ws[at, :], preferred_element_type=jnp.float32)
            value += jnp.dot(x, wv[at, :], preferred_element_type=jnp.float32)
        for full, dst in ((shared.astype(jnp.bfloat16), items_s), (value.astype(jnp.bfloat16), items_v)):
            for b in range(CH // BLK):
                for h in range(HG):
                    cols = slice(h * DH, (h + 1) * DH)
                    dst[(c * (CH // BLK) + b) * HG + h] = jnp.concatenate(
                        [full[b * BLK: b * BLK + BLK // 2, cols],
                         full[b * BLK + BLK // 2: (b + 1) * BLK, cols]], axis=1)

    for load in loads:
        load.wait()
    forward(0)

    def step(c, carry):
        forward(c)
        compute(c - 1)
        return carry

    lax.fori_loop(1, nc, step, 0)
    id2.wait_recv()
    id3.start()
    compute(nc - 1)
    id1.wait_recv()
    id3.wait_recv()
    ball[...] = ids[...]

    def drain(c, carry):
        over_x(c).wait_send()
        over_core(c).wait_send()
        onward(c).wait_send()
        return carry

    lax.fori_loop(0, nc, drain, 0)

    def bucket_drain(p, carry):
        bucket_copy(p).wait_send()
        return carry

    lax.fori_loop(1, n, bucket_drain, 0)
    id1.wait_send()
    id2.wait_send()
    id3.wait_send()


def attend_kernel(n, cap, nb, idx, items_s, items_v, tok, wo, out, s_out, v_out, s_in, v_in,
                  ts_out, ts_in, tv_out, tv_in, qbuf, kbuf, vbuf, wbuf, out2, ans,
                  sa, ra, sv, rv, st, rt, sr, rr, s1, r1, s2, r2, s3, r3):
    i = lax.axis_index("seq")
    g, h1, h2, h3 = head_ring()
    slots = n * cap
    at_pred, at_tail, at_target = slots, 2 * slots, 2 * slots + HG
    greet(n, i, g, h1, h2)

    def chunk(o):
        return pl.ds(o * cap, cap)

    def send_s(p):
        peer = lax.rem(i + p, n)
        return remote(s_out.at[peer], s_in.at[chunk(i)], sa.at[peer], ra.at[i], peer, g)

    def send_v(p):
        peer = lax.rem(i + p, n)
        return remote(v_out.at[peer], v_in.at[chunk(i)], sv.at[peer], rv.at[i], peer, g)

    def pack_s(p, carry):
        peer = lax.rem(i + p, n)
        for k in range(cap):
            s_out[peer, k] = items_s[idx[peer * cap + k]]
        send_s(p).start()
        return carry

    lax.fori_loop(1, n, pack_s, 0)

    def pack_v(p, carry):
        peer = lax.rem(i + p, n)
        for k in range(cap):
            v_out[peer, k] = items_v[idx[peer * cap + k]]
        return carry

    lax.fori_loop(1, n, pack_v, 0)
    for k in range(cap):
        s_in[i * cap + k] = items_s[idx[i * cap + k]]
        v_in[i * cap + k] = items_v[idx[i * cap + k]]

    low = lax.broadcasted_iota(jnp.int32, (BLK // 2, 2 * DH), 1) < DH
    query_scale = jnp.where(lax.broadcasted_iota(jnp.int32, (1, 2 * DH), 1) < DH,
                            jnp.float32(DH ** -0.5), jnp.float32(0.0))

    def unfold(x):
        x = x.astype(jnp.float32)
        turned = pltpu.roll(x, DH, 1)
        return jnp.concatenate([jnp.where(low, x, turned), jnp.where(low, turned, x)], axis=0)

    def khat_of(x):
        square = jnp.sum(x * x, axis=1, keepdims=True) * (0.5 / DH)
        return (x * lax.rsqrt(square + 1e-6)).astype(jnp.bfloat16)

    def ready_s(o):
        for k in range(cap):
            j = o * cap + k
            x = unfold(s_in[j])
            qbuf[j] = (x * query_scale).astype(jnp.bfloat16)
            kbuf[j] = khat_of(x)

    def ready_v(o):
        for k in range(cap):
            j = o * cap + k
            vbuf[j] = unfold(v_in[j]).astype(jnp.bfloat16)

    ready_s(i)

    def arrive_s(p, carry):
        src = lax.rem(i + n - p, n)
        remote(s_out.at[src], s_in.at[chunk(src)], sa.at[src], ra.at[src], src, g).wait_recv()
        send_v(p).start()
        ready_s(src)
        return carry

    lax.fori_loop(1, n, arrive_s, 0)
    for h in range(HG):
        ts_out[h] = s_in[idx[at_tail + h]]
    following = lax.rem(i + 1, n)
    tail_s = remote(ts_out, ts_in, st.at[0], rt.at[0], following, g)
    tail_s.start()
    ready_v(i)
    tail_s.wait_recv()
    for h in range(HG):
        kbuf[slots + h] = khat_of(unfold(ts_in[h]))

    row_at = lax.broadcasted_iota(jnp.int32, (BLK, 2 * BLK), 0)
    col_at = lax.broadcasted_iota(jnp.int32, (BLK, 2 * BLK), 1)
    itself = col_at == row_at + BLK

    def weigh(o, carry):
        for k in range(cap):
            j = o * cap + k
            keys = jnp.concatenate([kbuf[idx[at_pred + j]], kbuf[j]], axis=0)
            scores = lax.dot_general(qbuf[j], keys, (((1,), (1,)), ((), ())),
                                     preferred_element_type=jnp.float32)
            scores = jnp.where(itself, jnp.float32(-100000.0), scores)
            expo = jnp.exp(scores - jnp.max(scores, axis=1, keepdims=True))
            wbuf[j] = (expo * (1.0 / jnp.sum(expo, axis=1, keepdims=True))).astype(jnp.bfloat16)
        return carry

    lax.fori_loop(0, n, weigh, 0)

    def arrive_v(p, carry):
        src = lax.rem(i + n - p, n)
        remote(v_out.at[src], v_in.at[chunk(src)], sv.at[src], rv.at[src], src, g).wait_recv()
        ready_v(src)
        return carry

    lax.fori_loop(1, n, arrive_v, 0)
    for h in range(HG):
        tv_out[h] = v_in[idx[at_tail + h]]
    tail_v = remote(tv_out, tv_in, st.at[1], rt.at[1], following, g)
    tail_v.start()
    tail_v.wait_recv()
    for h in range(HG):
        vbuf[slots + h] = unfold(tv_in[h]).astype(jnp.bfloat16)

    def attend(j):
        values = jnp.concatenate([vbuf[idx[at_pred + j]], vbuf[j]], axis=0)
        mixed = jnp.dot(wbuf[j], values, preferred_element_type=jnp.float32)
        return jnp.where(low, mixed[: BLK // 2], mixed[BLK // 2:]).astype(jnp.bfloat16)

    def reply(p):
        peer = lax.rem(i + p, n)
        return remote(out2.at[peer], ans.at[0, chunk(i)], sr.at[peer], rr.at[i], peer, g)

    def relay1(o):
        return remote(ans.at[0, chunk(o)], ans.at[1, chunk(o)], s1.at[o], r1.at[o], i, h1)

    def relay2(o):
        return remote(ans.at[0, chunk(o)], ans.at[2, chunk(o)], s2.at[o], r2.at[o], i, h2)

    def relay3(o):
        return remote(ans.at[2, chunk(o)], ans.at[3, chunk(o)], s3.at[o], r3.at[o], i, h1)

    for k in range(cap):
        ans[0, i * cap + k] = attend(i * cap + k)
    relay2(i).start()
    relay1(i).start()

    def stride(t):
        return n // 2 + lax.div(t + 1, 2) * (1 - 2 * lax.rem(t, 2))

    def answer(t):
        p = stride(t)
        peer = lax.rem(i + p, n)
        for k in range(cap):
            out2[peer, k] = attend(peer * cap + k)
        reply(p).start()

    def relay(t):
        src = lax.rem(i + n - stride(t), n)
        remote(out2.at[src], ans.at[0, chunk(src)], sr.at[src], rr.at[src], src, g).wait_recv()
        relay2(src).start()
        relay1(src).start()

    def spread(t):
        src = lax.rem(i + n - stride(t), n)
        relay2(src).wait_recv()
        relay3(src).start()

    ahead = 2
    for t in range(ahead):
        answer(t)
    relay2(i).wait_recv()
    relay3(i).start()

    def flow(t, carry):
        answer(t)
        relay(t - ahead)

        @pl.when(t > ahead)
        def _():
            spread(t - ahead - 1)
        return carry

    lax.fori_loop(ahead, n - 1, flow, 0)
    for t in range(n - 1 - ahead, n - 1):
        relay(t)
        spread(t - 1)
    spread(n - 2)

    def settle(o, carry):
        relay1(o).wait_recv()
        relay3(o).wait_recv()
        return carry

    lax.fori_loop(0, n, settle, 0)

    group = 4

    def finish(q, carry):
        total = jnp.zeros((group * BLK, wo.shape[1]), jnp.float32)
        for r, h in enumerate((g, h1, h2, h3)):
            rows = []
            for b in range(group):
                at = at_target + (r * nb + q * group + b) * HG
                parts = [ans[r, idx[at + k]] for k in range(HG)]
                rows.append(jnp.concatenate([x[:, :DH] for x in parts], axis=1))
                rows.append(jnp.concatenate([x[:, DH:] for x in parts], axis=1))
            total += jnp.dot(jnp.concatenate(rows, axis=0),
                             wo[pl.ds(pl.multiple_of(h * HG * DH, HG * DH), HG * DH), :],
                             preferred_element_type=jnp.float32)
        at = pl.ds(q * group, group)
        base = tok[at].reshape(group * BLK, -1).astype(jnp.float32)
        out[at] = (base + total).astype(jnp.bfloat16).reshape(group, BLK, -1)
        return carry

    lax.fori_loop(0, nb // group, finish, 0)

    def drain(p, carry):
        send_s(p).wait_send()
        send_v(p).wait_send()
        reply(p).wait_send()
        return carry

    lax.fori_loop(1, n, drain, 0)
    tail_s.wait_send()
    tail_v.wait_send()

    def drain_relays(o, carry):
        relay1(o).wait_send()
        relay2(o).wait_send()
        relay3(o).wait_send()
        return carry

    lax.fori_loop(0, n, drain_relays, 0)


def index_tables(ball, n, nb, cap):
    i = lax.axis_index("seq")
    blocks, slots = n * nb, n * cap
    key = ball[..., :HG].reshape(HG, blocks, HG) * blocks + jnp.arange(blocks, dtype=jnp.int32)[None, :, None]
    key = jnp.transpose(key, (0, 2, 1))
    position = jnp.sum((key[:, :, None, :] < key[:, :, :, None]).astype(jnp.int32), axis=3)
    position = jnp.transpose(position, (0, 2, 1)).reshape(HG, n, nb * HG)
    count = nb * HG
    item = jnp.arange(count, dtype=jnp.int32)
    owner, within = position // nb, position % nb
    same = owner[..., :, None] == owner[..., None, :]
    slot = jnp.sum((same & (item[None, :] < item[:, None])).astype(jnp.int32), axis=3)
    target = lax.dynamic_index_in_dim(owner * cap + slot, i, 1, keepdims=False)
    slot_ids = jnp.arange(slots, dtype=jnp.int32)
    inverse = jnp.sum(jnp.where(target[0][None, :] == slot_ids[:, None], item[None, :], 0), axis=1)
    place = (jnp.arange(n, dtype=jnp.int32)[:, None] * cap + slot[0]).reshape(-1)
    mine = (owner[0] == i).reshape(-1)
    grid = ((item % HG)[None, :] * nb + within[0]).reshape(-1)
    grid_of = jnp.sum(jnp.where(mine & (place == slot_ids[:, None]), grid, 0), axis=1)
    slot_of = jnp.sum(jnp.where(mine & (grid == item[:, None]), place, 0), axis=1)
    inside = jnp.sum(jnp.where(item[None, :] == grid_of[:, None] - 1, slot_of[None, :], 0), axis=1)
    before = jnp.where(grid_of % nb == 0, slots + grid_of // nb, inside)
    tails = slot_of.reshape(HG, nb)[:, nb - 1]
    return jnp.concatenate([inverse, before, tails, target.reshape(-1)]).astype(jnp.int32)


def per_device(tokens, buckets, w_shared, w_value, w_output):
    n = lax.axis_size("seq")
    nb = buckets.shape[0]
    rows, width = tokens.shape
    cap = max(1, nb * HG // n)
    nc = rows // CH
    vmem = pl.BlockSpec(memory_space=pltpu.VMEM)
    dma = lambda k: pltpu.SemaphoreType.DMA((k,))
    bf = jnp.bfloat16
    padded = jnp.pad(buckets, ((0, 0), (0, 128 - HG)))
    hbm = pl.BlockSpec(memory_space=pltpu.HBM)
    half = (BLK // 2, 2 * DH)
    items_s, items_v, ball = pl.pallas_call(
        functools.partial(project_kernel, n, nc),
        out_shape=(jax.ShapeDtypeStruct((nb * HG,) + half, bf),
                   jax.ShapeDtypeStruct((nb * HG,) + half, bf),
                   jax.ShapeDtypeStruct((HG, n, nb, 128), jnp.int32)),
        in_specs=[hbm, vmem, hbm, hbm],
        out_specs=(vmem, vmem, vmem),
        scratch_shapes=[pltpu.VMEM((nc, CH, width), bf), pltpu.VMEM(w_shared.shape, bf), pltpu.VMEM(w_value.shape, bf)]
        + [pltpu.VMEM((nc, CH, width), bf)] * 3
        + [pltpu.VMEM((HG, n, nb, 128), jnp.int32)]
        + [dma(3)] + [dma(nc)] * 6 + [dma(n), dma(n), dma(3), dma(3)],
        compiler_params=pltpu.CompilerParams(collective_id=0, has_side_effects=True,
                                             vmem_limit_bytes=40 << 20),
    )(tokens.reshape(nc, CH, width), padded, w_shared, w_value)
    idx = index_tables(ball, n, nb, cap)
    slots = n * cap
    out = pl.pallas_call(
        functools.partial(attend_kernel, n, cap, nb),
        out_shape=jax.ShapeDtypeStruct((nb, BLK, width), bf),
        in_specs=[pl.BlockSpec(memory_space=pltpu.SMEM)] + [vmem] * 4,
        out_specs=vmem,
        scratch_shapes=[pltpu.VMEM((n, cap) + half, bf)] * 2
        + [pltpu.VMEM((slots,) + half, bf)] * 2
        + [pltpu.VMEM((HG,) + half, bf)] * 4
        + [pltpu.VMEM((slots, BLK, 2 * DH), bf)]
        + [pltpu.VMEM((slots + HG, BLK, 2 * DH), bf)] * 2
        + [pltpu.VMEM((slots, BLK, 2 * BLK), bf)]
        + [pltpu.VMEM((n, cap) + half, bf), pltpu.VMEM((HG, slots) + half, bf)]
        + [dma(n)] * 4 + [dma(2)] * 2 + [dma(n)] * 8,
        compiler_params=pltpu.CompilerParams(collective_id=1, has_side_effects=True,
                                             vmem_limit_bytes=48 << 20),
    )(idx, items_s, items_v, tokens.reshape(nb, BLK, width), w_output)
    return out.reshape(rows, width)


def solution(mesh):
    return jax.shard_map(
        per_device,
        mesh=mesh,
        in_specs=(
            P("seq", "head"),
            P("seq", "head"),
            P(None, "head"),
            P(None, "head"),
            P(None, "head"),
        ),
        out_specs=P("seq", "head"),
        check_vma=False,
    )
```

```python
import functools

import jax
import jax.numpy as jnp
from jax import lax
from jax.experimental import pallas as pl
from jax.experimental.pallas import tpu as pltpu
from jax.sharding import PartitionSpec as P

DH = 64
BLK = 128
HG = 4
CH = 256
MESH = pl.DeviceIdType.MESH


def head_ring():
    g = lax.axis_index("head")
    h1 = g + 1 - 2 * lax.rem(g, 2)
    h2 = g + 2 - 4 * lax.div(g, 2)
    h3 = h1 + 2 - 4 * lax.div(h1, 2)
    return g, h1, h2, h3


def remote(src, dst, send, recv, seq, head):
    return pltpu.make_async_remote_copy(
        src_ref=src, dst_ref=dst, send_sem=send, recv_sem=recv,
        device_id=(seq, head), device_id_type=MESH,
    )


def greet(n, i, g, h1, h2):
    barrier = pltpu.get_barrier_semaphore()

    def say(p, c):
        pl.semaphore_signal(barrier, inc=1, device_id=(lax.rem(i + p, n), g), device_id_type=MESH)
        return c

    lax.fori_loop(1, n, say, 0)
    for h in (h1, h2):
        pl.semaphore_signal(barrier, inc=1, device_id=(i, h), device_id_type=MESH)
    pl.semaphore_wait(barrier, n + 1)


def project_kernel(n, nc, tok, buck, ws_hbm, wv_hbm, items_s, items_v, ball, own, ws, wv, g1, g2, g3, ids,
                   local, s1, r1, s2, r2, s3, r3, sb, rb, sh, rh):
    i = lax.axis_index("seq")
    g, h1, h2, h3 = head_ring()
    loads = [pltpu.make_async_copy(src, dst, local.at[k])
             for k, (src, dst) in enumerate(((tok, own), (ws_hbm, ws), (wv_hbm, wv)))]
    for load in loads:
        load.start()
    greet(n, i, g, h1, h2)

    def over_x(c):
        return remote(tok.at[c], g2.at[c], s2.at[c], r2.at[c], i, h2)

    def over_core(c):
        return remote(tok.at[c], g1.at[c], s1.at[c], r1.at[c], i, h1)

    def onward(c):
        return remote(g2.at[c], g3.at[c], s3.at[c], r3.at[c], i, h1)

    def launch(c, carry):
        over_x(c).start()
        over_core(c).start()
        return carry

    lax.fori_loop(0, nc, launch, 0)
    ids[0, i] = buck[...]

    def bucket_copy(p):
        peer = lax.rem(i + p, n)
        return remote(buck, ids.at[0, i], sb.at[peer], rb.at[i], peer, g)

    def bucket_start(p, carry):
        bucket_copy(p).start()
        return carry

    lax.fori_loop(1, n, bucket_start, 0)

    def bucket_wait(p, carry):
        src = lax.rem(i + n - p, n)
        remote(buck, ids.at[0, src], sb.at[src], rb.at[src], src, g).wait_recv()
        return carry

    lax.fori_loop(1, n, bucket_wait, 0)
    id1 = remote(ids.at[0], ids.at[1], sh.at[0], rh.at[0], i, h1)
    id2 = remote(ids.at[0], ids.at[2], sh.at[1], rh.at[1], i, h2)
    id3 = remote(ids.at[2], ids.at[3], sh.at[2], rh.at[2], i, h1)
    id1.start()
    id2.start()

    def forward(c):
        over_x(c).wait_recv()
        onward(c).start()

    def compute(c):
        over_core(c).wait_recv()
        onward(c).wait_recv()
        shared = jnp.zeros((CH, HG * DH), jnp.float32)
        value = jnp.zeros((CH, HG * DH), jnp.float32)
        for ref, h in ((own, g), (g1, h1), (g2, h2), (g3, h3)):
            x = ref[c]
            at = pl.ds(pl.multiple_of(h * CH, CH), CH)
            shared += jnp.dot(x, ws[at, :], preferred_element_type=jnp.float32)
            value += jnp.dot(x, wv[at, :], preferred_element_type=jnp.float32)
        for full, dst in ((shared.astype(jnp.bfloat16), items_s), (value.astype(jnp.bfloat16), items_v)):
            for b in range(CH // BLK):
                for h in range(HG):
                    cols = slice(h * DH, (h + 1) * DH)
                    dst[(c * (CH // BLK) + b) * HG + h] = jnp.concatenate(
                        [full[b * BLK: b * BLK + BLK // 2, cols],
                         full[b * BLK + BLK // 2: (b + 1) * BLK, cols]], axis=1)

    for load in loads:
        load.wait()
    forward(0)

    def step(c, carry):
        forward(c)
        compute(c - 1)
        return carry

    lax.fori_loop(1, nc, step, 0)
    id2.wait_recv()
    id3.start()
    compute(nc - 1)
    id1.wait_recv()
    id3.wait_recv()
    ball[...] = ids[...]

    def drain(c, carry):
        over_x(c).wait_send()
        over_core(c).wait_send()
        onward(c).wait_send()
        return carry

    lax.fori_loop(0, nc, drain, 0)

    def bucket_drain(p, carry):
        bucket_copy(p).wait_send()
        return carry

    lax.fori_loop(1, n, bucket_drain, 0)
    id1.wait_send()
    id2.wait_send()
    id3.wait_send()


def attend_kernel(n, cap, nb, idx, items_s, items_v, tok, wo, out, s_out, v_out, s_in, v_in,
                  ts_out, ts_in, tv_out, tv_in, qbuf, kbuf, vbuf, wbuf, out2, ans,
                  sa, ra, sv, rv, st, rt, sr, rr, s1, r1, s2, r2, s3, r3):
    i = lax.axis_index("seq")
    g, h1, h2, h3 = head_ring()
    slots = n * cap
    at_pred, at_tail, at_target = slots, 2 * slots, 2 * slots + HG
    greet(n, i, g, h1, h2)

    def chunk(o):
        return pl.ds(o * cap, cap)

    def send_s(p):
        peer = lax.rem(i + p, n)
        return remote(s_out.at[peer], s_in.at[chunk(i)], sa.at[peer], ra.at[i], peer, g)

    def send_v(p):
        peer = lax.rem(i + p, n)
        return remote(v_out.at[peer], v_in.at[chunk(i)], sv.at[peer], rv.at[i], peer, g)

    def pack_s(p, carry):
        peer = lax.rem(i + p, n)
        for k in range(cap):
            s_out[peer, k] = items_s[idx[peer * cap + k]]
        send_s(p).start()
        return carry

    lax.fori_loop(1, n, pack_s, 0)

    def pack_v(p, carry):
        peer = lax.rem(i + p, n)
        for k in range(cap):
            v_out[peer, k] = items_v[idx[peer * cap + k]]
        return carry

    lax.fori_loop(1, n, pack_v, 0)
    for k in range(cap):
        s_in[i * cap + k] = items_s[idx[i * cap + k]]
        v_in[i * cap + k] = items_v[idx[i * cap + k]]

    low = lax.broadcasted_iota(jnp.int32, (BLK // 2, 2 * DH), 1) < DH
    query_scale = jnp.where(lax.broadcasted_iota(jnp.int32, (1, 2 * DH), 1) < DH,
                            jnp.float32(DH ** -0.5), jnp.float32(0.0))

    def unfold(x):
        x = x.astype(jnp.float32)
        turned = pltpu.roll(x, DH, 1)
        return jnp.concatenate([jnp.where(low, x, turned), jnp.where(low, turned, x)], axis=0)

    def khat_of(x):
        square = jnp.sum(x * x, axis=1, keepdims=True) * (0.5 / DH)
        return (x * lax.rsqrt(square + 1e-6)).astype(jnp.bfloat16)

    def ready_s(o):
        for k in range(cap):
            j = o * cap + k
            x = unfold(s_in[j])
            qbuf[j] = (x * query_scale).astype(jnp.bfloat16)
            kbuf[j] = khat_of(x)

    def ready_v(o):
        for k in range(cap):
            j = o * cap + k
            vbuf[j] = unfold(v_in[j]).astype(jnp.bfloat16)

    ready_s(i)

    def arrive_s(p, carry):
        src = lax.rem(i + n - p, n)
        remote(s_out.at[src], s_in.at[chunk(src)], sa.at[src], ra.at[src], src, g).wait_recv()
        send_v(p).start()
        ready_s(src)
        return carry

    lax.fori_loop(1, n, arrive_s, 0)
    for h in range(HG):
        ts_out[h] = s_in[idx[at_tail + h]]
    following = lax.rem(i + 1, n)
    tail_s = remote(ts_out, ts_in, st.at[0], rt.at[0], following, g)
    tail_s.start()
    ready_v(i)
    tail_s.wait_recv()
    for h in range(HG):
        kbuf[slots + h] = khat_of(unfold(ts_in[h]))

    row_at = lax.broadcasted_iota(jnp.int32, (BLK, 2 * BLK), 0)
    col_at = lax.broadcasted_iota(jnp.int32, (BLK, 2 * BLK), 1)
    itself = col_at == row_at + BLK

    def weigh(o, carry):
        for k in range(cap):
            j = o * cap + k
            keys = jnp.concatenate([kbuf[idx[at_pred + j]], kbuf[j]], axis=0)
            scores = lax.dot_general(qbuf[j], keys, (((1,), (1,)), ((), ())),
                                     preferred_element_type=jnp.float32)
            scores = jnp.where(itself, jnp.float32(-100000.0), scores)
            expo = jnp.exp(scores - jnp.max(scores, axis=1, keepdims=True))
            wbuf[j] = (expo * (1.0 / jnp.sum(expo, axis=1, keepdims=True))).astype(jnp.bfloat16)
        return carry

    lax.fori_loop(0, n, weigh, 0)

    def arrive_v(p, carry):
        src = lax.rem(i + n - p, n)
        remote(v_out.at[src], v_in.at[chunk(src)], sv.at[src], rv.at[src], src, g).wait_recv()
        ready_v(src)
        return carry

    lax.fori_loop(1, n, arrive_v, 0)
    for h in range(HG):
        tv_out[h] = v_in[idx[at_tail + h]]
    tail_v = remote(tv_out, tv_in, st.at[1], rt.at[1], following, g)
    tail_v.start()
    tail_v.wait_recv()
    for h in range(HG):
        vbuf[slots + h] = unfold(tv_in[h]).astype(jnp.bfloat16)

    def attend(j):
        values = jnp.concatenate([vbuf[idx[at_pred + j]], vbuf[j]], axis=0)
        mixed = jnp.dot(wbuf[j], values, preferred_element_type=jnp.float32)
        return jnp.where(low, mixed[: BLK // 2], mixed[BLK // 2:]).astype(jnp.bfloat16)

    def reply(p):
        peer = lax.rem(i + p, n)
        return remote(out2.at[peer], ans.at[0, chunk(i)], sr.at[peer], rr.at[i], peer, g)

    def relay1(o):
        return remote(ans.at[0, chunk(o)], ans.at[1, chunk(o)], s1.at[o], r1.at[o], i, h1)

    def relay2(o):
        return remote(ans.at[0, chunk(o)], ans.at[2, chunk(o)], s2.at[o], r2.at[o], i, h2)

    def relay3(o):
        return remote(ans.at[2, chunk(o)], ans.at[3, chunk(o)], s3.at[o], r3.at[o], i, h1)

    for k in range(cap):
        ans[0, i * cap + k] = attend(i * cap + k)
    relay2(i).start()
    relay1(i).start()

    def stride(t):
        odd = lax.rem(t, 2)
        return (1 - odd) * (lax.div(t, 2) + 1) + odd * (n - lax.div(t + 1, 2))

    def answer(t):
        p = stride(t)
        peer = lax.rem(i + p, n)
        for k in range(cap):
            out2[peer, k] = attend(peer * cap + k)
        reply(p).start()

    def relay(t):
        src = lax.rem(i + n - stride(t), n)
        remote(out2.at[src], ans.at[0, chunk(src)], sr.at[src], rr.at[src], src, g).wait_recv()
        relay2(src).start()
        relay1(src).start()

    def spread(t):
        src = lax.rem(i + n - stride(t), n)
        relay2(src).wait_recv()
        relay3(src).start()

    ahead = 3
    for t in range(ahead):
        answer(t)
    relay2(i).wait_recv()
    relay3(i).start()

    def flow(t, carry):
        answer(t)
        relay(t - ahead)

        @pl.when(t > ahead)
        def _():
            spread(t - ahead - 1)
        return carry

    lax.fori_loop(ahead, n - 1, flow, 0)
    for t in range(n - 1 - ahead, n - 1):
        relay(t)
        spread(t - 1)
    spread(n - 2)

    def settle(o, carry):
        relay1(o).wait_recv()
        relay3(o).wait_recv()
        return carry

    lax.fori_loop(0, n, settle, 0)

    group = 4

    def finish(q, carry):
        total = jnp.zeros((group * BLK, wo.shape[1]), jnp.float32)
        for r, h in enumerate((g, h1, h2, h3)):
            rows = []
            for b in range(group):
                at = at_target + (r * nb + q * group + b) * HG
                parts = [ans[r, idx[at + k]] for k in range(HG)]
                rows.append(jnp.concatenate([x[:, :DH] for x in parts], axis=1))
                rows.append(jnp.concatenate([x[:, DH:] for x in parts], axis=1))
            total += jnp.dot(jnp.concatenate(rows, axis=0),
                             wo[pl.ds(pl.multiple_of(h * HG * DH, HG * DH), HG * DH), :],
                             preferred_element_type=jnp.float32)
        at = pl.ds(q * group, group)
        base = tok[at].reshape(group * BLK, -1).astype(jnp.float32)
        out[at] = (base + total).astype(jnp.bfloat16).reshape(group, BLK, -1)
        return carry

    lax.fori_loop(0, nb // group, finish, 0)

    def drain(p, carry):
        send_s(p).wait_send()
        send_v(p).wait_send()
        reply(p).wait_send()
        return carry

    lax.fori_loop(1, n, drain, 0)
    tail_s.wait_send()
    tail_v.wait_send()

    def drain_relays(o, carry):
        relay1(o).wait_send()
        relay2(o).wait_send()
        relay3(o).wait_send()
        return carry

    lax.fori_loop(0, n, drain_relays, 0)


def index_tables(ball, n, nb, cap):
    i = lax.axis_index("seq")
    blocks, slots = n * nb, n * cap
    key = ball[..., :HG].reshape(HG, blocks, HG) * blocks + jnp.arange(blocks, dtype=jnp.int32)[None, :, None]
    key = jnp.transpose(key, (0, 2, 1))
    position = jnp.sum((key[:, :, None, :] < key[:, :, :, None]).astype(jnp.int32), axis=3)
    position = jnp.transpose(position, (0, 2, 1)).reshape(HG, n, nb * HG)
    count = nb * HG
    item = jnp.arange(count, dtype=jnp.int32)
    owner, within = position // nb, position % nb
    earlier = item[None, :] < item[:, None]

    def slot_in(owners):
        same = owners[:, :, None] == owners[:, None, :]
        return jnp.sum((same & earlier).astype(jnp.int32), axis=2)

    here = lax.dynamic_index_in_dim(owner, i, 1, keepdims=False)
    target = here * cap + slot_in(here)
    slot_ids = jnp.arange(slots, dtype=jnp.int32)
    inverse = jnp.sum(jnp.where(target[0][None, :] == slot_ids[:, None], item[None, :], 0), axis=1)
    place = (jnp.arange(n, dtype=jnp.int32)[:, None] * cap + slot_in(owner[0])).reshape(-1)
    mine = (owner[0] == i).reshape(-1)
    grid = ((item % HG)[None, :] * nb + within[0]).reshape(-1)
    grid_of = jnp.sum(jnp.where(mine & (place == slot_ids[:, None]), grid, 0), axis=1)
    slot_of = jnp.sum(jnp.where(mine & (grid == item[:, None]), place, 0), axis=1)
    inside = jnp.sum(jnp.where(item[None, :] == grid_of[:, None] - 1, slot_of[None, :], 0), axis=1)
    before = jnp.where(grid_of % nb == 0, slots + grid_of // nb, inside)
    tails = slot_of.reshape(HG, nb)[:, nb - 1]
    return jnp.concatenate([inverse, before, tails, target.reshape(-1)]).astype(jnp.int32)


def per_device(tokens, buckets, w_shared, w_value, w_output):
    n = lax.axis_size("seq")
    nb = buckets.shape[0]
    rows, width = tokens.shape
    cap = max(1, nb * HG // n)
    nc = rows // CH
    vmem = pl.BlockSpec(memory_space=pltpu.VMEM)
    dma = lambda k: pltpu.SemaphoreType.DMA((k,))
    bf = jnp.bfloat16
    padded = jnp.pad(buckets, ((0, 0), (0, 128 - HG)))
    hbm = pl.BlockSpec(memory_space=pltpu.HBM)
    half = (BLK // 2, 2 * DH)
    items_s, items_v, ball = pl.pallas_call(
        functools.partial(project_kernel, n, nc),
        out_shape=(jax.ShapeDtypeStruct((nb * HG,) + half, bf),
                   jax.ShapeDtypeStruct((nb * HG,) + half, bf),
                   jax.ShapeDtypeStruct((HG, n, nb, 128), jnp.int32)),
        in_specs=[hbm, vmem, hbm, hbm],
        out_specs=(vmem, vmem, vmem),
        scratch_shapes=[pltpu.VMEM((nc, CH, width), bf), pltpu.VMEM(w_shared.shape, bf), pltpu.VMEM(w_value.shape, bf)]
        + [pltpu.VMEM((nc, CH, width), bf)] * 3
        + [pltpu.VMEM((HG, n, nb, 128), jnp.int32)]
        + [dma(3)] + [dma(nc)] * 6 + [dma(n), dma(n), dma(3), dma(3)],
        compiler_params=pltpu.CompilerParams(collective_id=0, has_side_effects=True,
                                             vmem_limit_bytes=40 << 20),
    )(tokens.reshape(nc, CH, width), padded, w_shared, w_value)
    idx = index_tables(ball, n, nb, cap)
    slots = n * cap
    out = pl.pallas_call(
        functools.partial(attend_kernel, n, cap, nb),
        out_shape=jax.ShapeDtypeStruct((nb, BLK, width), bf),
        in_specs=[pl.BlockSpec(memory_space=pltpu.SMEM)] + [vmem] * 4,
        out_specs=vmem,
        scratch_shapes=[pltpu.VMEM((n, cap) + half, bf)] * 2
        + [pltpu.VMEM((slots,) + half, bf)] * 2
        + [pltpu.VMEM((HG,) + half, bf)] * 4
        + [pltpu.VMEM((slots, BLK, 2 * DH), bf)]
        + [pltpu.VMEM((slots + HG, BLK, 2 * DH), bf)] * 2
        + [pltpu.VMEM((slots, BLK, 2 * BLK), bf)]
        + [pltpu.VMEM((n, cap) + half, bf), pltpu.VMEM((HG, slots) + half, bf)]
        + [dma(n)] * 4 + [dma(2)] * 2 + [dma(n)] * 8,
        compiler_params=pltpu.CompilerParams(collective_id=1, has_side_effects=True,
                                             vmem_limit_bytes=48 << 20),
    )(idx, items_s, items_v, tokens.reshape(nb, BLK, width), w_output)
    return out.reshape(rows, width)


def solution(mesh):
    return jax.shard_map(
        per_device,
        mesh=mesh,
        in_specs=(
            P("seq", "head"),
            P("seq", "head"),
            P(None, "head"),
            P(None, "head"),
            P(None, "head"),
        ),
        out_specs=P("seq", "head"),
        check_vma=False,
    )
```
